256 devices in a mesh: depth: 4 (over z_hi), row: 16 (over x, y), col: 4 (over z_lo, core).
Axes of the slice: x: 4, y: 4, z: 8 (z_hi: 4, z_lo: 2; z = z_hi * 2 + z_lo), core: 2. Of those that a mesh axis runs over, the one named last changes fastest.
Arguments:
- tokens: bfloat16 [1536, 8192], P('row', ('depth', 'col')), may hold values from -6 to 6
- cotangent: bfloat16 [1536, 8192], P('row', ('depth', 'col')), may hold values from -0.95703125 to 0.95703125
- gate_weight: bfloat16 [8192, 14336], P(('depth', 'col'), 'row'), may hold values from -0.0625 to 0.0625
- up_weight: bfloat16 [8192, 14336], P(('depth', 'col'), 'row'), may hold values from -0.0625 to 0.0625
- down_weight: bfloat16 [14336, 8192], P('row', ('depth', 'col')), may hold values from -0.046875 to 0.046875
Outputs:
- input_grad: bfloat16 [1536, 8192], P('row', ('depth', 'col'))
- gate_grad: bfloat16 [8192, 14336], P(('depth', 'col'), 'row')
- up_grad: bfloat16 [8192, 14336], P(('depth', 'col'), 'row')
- down_grad: bfloat16 [14336, 8192], P('row', ('depth', 'col'))
The draws below stay inside these ranges and needn't reach their ends.
All inputs are finite; a program needn't handle non-finite values.
Results may differ from the reference program's by a relative error of at most 0.0065.
Values may be sent and summed in bfloat16 or wider, within the bound.
A program may use at most 128 MiB of HBM per device.

```python
import jax
import jax.numpy as jnp
from jax import lax

D = 8192
FF = 14336
TOKENS = 1536


def block_levels(stream_key, dims, shards, smallest, largest):
    factor_of = 1.0
    for dim, parts in shards:
        heights = jax.random.uniform(jax.random.fold_in(jax.random.fold_in(stream_key, 6), dim), (parts,), jnp.float32, smallest / len(shards), largest / len(shards))
        factor_of = factor_of * jnp.repeat(jnp.exp(heights), dims[dim] // parts).reshape((-1,) + (1,) * (len(dims) - 1 - dim))
    return factor_of


def centred(stream_key, dims, width, bound, pieces=(), kind=jnp.bfloat16):
    array = width * jax.random.normal(stream_key, dims, jnp.float32)
    if pieces:
        array = array * block_levels(stream_key, dims, pieces, -0.22, 0.18)
    return jnp.clip(array, -bound, bound).astype(kind)


def setup_inputs(seed: int = 0) -> dict:
    arg_keys = jax.random.split(jax.random.key(seed), 6)
    return {
        "tokens": centred(arg_keys[0], (TOKENS, D), 1.0, 6.0, ((0, 16), (1, 16))),
        "cotangent": centred(arg_keys[1], (TOKENS, D), (TOKENS ** -0.25), 0.95703125, ((0, 16), (1, 16))),
        "gate_weight": centred(arg_keys[2], (D, FF), D ** -0.5, 0.0625, ((0, 16), (1, 16))),
        "up_weight": centred(arg_keys[3], (D, FF), D ** -0.5, 0.0625, ((0, 16), (1, 16))),
        "down_weight": centred(arg_keys[4], (FF, D), FF ** -0.5, 0.046875, ((0, 16), (1, 16))),
    }


def reference(tokens, cotangent, gate_weight, up_weight, down_weight):
    gate = jnp.dot(tokens, gate_weight, preferred_element_type=jnp.float32)
    up = jnp.dot(tokens, up_weight, preferred_element_type=jnp.float32)
    back = lax.dot_general(cotangent, down_weight, (((1,), (1,)), ((), ())), preferred_element_type=jnp.float32)
    sig = jax.nn.sigmoid(gate)
    hidden = (gate * sig * up).astype(jnp.bfloat16)
    grad_gate = (back * up * sig * (1.0 + gate * (1.0 - sig))).astype(jnp.bfloat16)
    grad_up = (back * gate * sig).astype(jnp.bfloat16)
    input_grad = lax.dot_general(grad_gate, gate_weight, (((1,), (1,)), ((), ())), preferred_element_type=jnp.float32)
    input_grad = input_grad + lax.dot_general(grad_up, up_weight, (((1,), (1,)), ((), ())), preferred_element_type=jnp.float32)
    gate_grad = lax.dot_general(tokens, grad_gate, (((0,), (0,)), ((), ())), preferred_element_type=jnp.float32)
    up_grad = lax.dot_general(tokens, grad_up, (((0,), (0,)), ((), ())), preferred_element_type=jnp.float32)
    down_grad = lax.dot_general(hidden, cotangent, (((0,), (0,)), ((), ())), preferred_element_type=jnp.float32)
    return (input_grad.astype(jnp.bfloat16), gate_grad.astype(jnp.bfloat16),
            up_grad.astype(jnp.bfloat16), down_grad.astype(jnp.bfloat16))
```

```python
import jax
import jax.numpy as jnp
from jax import lax
from jax.experimental import pallas as pl
from jax.experimental.pallas import tpu as pltpu
from jax.sharding import PartitionSpec as P

MESH = pl.DeviceIdType.MESH
BF16 = jnp.bfloat16
F32 = jnp.float32

STAGES = 6
ROWS = 128
CHUNK = 16
BLOCK = 48
HALF = STAGES * ROWS


def shift(dx, n):
    b = dx
    return b + b // 2 - n // 2 * (b // 3)


def kernel(
    tok, cot, wg, wu, wd,
    ig_out, gg_out, gu_out, gd_out,
    tc, tx, wgu, wdn, wgux, wdnx, q, sl, rl, ss, rs, hid, acc, accd, igb, igr,
    loc_sem, w_send, w_recv, a_send, a_recv, x_send, x_recv,
    ring_send, rl_recv, rs_recv, al_recv, as_recv, pf_send, pf_recv, ig_send, ig_recv,
):
    ff = wg.shape[1]
    depth, row, col = lax.axis_index("depth"), lax.axis_index("row"), lax.axis_index("col")
    x, y = row // 4, row % 4
    z, core = depth * 2 + col // 2, col % 2
    sign = 1 - 2 * core

    def at(xx, yy, zz, cc):
        return (zz // 2, xx * 4 + yy, (zz % 2) * 2 + cc)

    def plane(dx, dy):
        return at((x + dx) % 4, (y + dy) % 4, z, core)

    partner = at(x, y, z, 1 - core)
    far = at(x, y, (z + sign + 8) % 8, core)
    near = at(x, y, (z - sign + 8) % 8, core)

    def remote(src, dst, send, recv, device):
        return pltpu.make_async_remote_copy(
            src_ref=src, dst_ref=dst, send_sem=send, recv_sem=recv,
            device_id=device, device_id_type=MESH,
        )

    local = [
        pltpu.make_async_copy(src.at[pl.ds(BLOCK * half, BLOCK)], tc.at[t, half, pl.ds(0, BLOCK)], loc_sem.at[2 * t + half])
        for t, src in enumerate((tok, cot))
        for half in range(2)
    ]
    local += [
        pltpu.make_async_copy(wg, wgu.at[0], loc_sem.at[4]),
        pltpu.make_async_copy(wu, wgu.at[1], loc_sem.at[5]),
        pltpu.make_async_copy(wd, wdn, loc_sem.at[6]),
    ]
    for copy in local:
        copy.start()
    barrier = pltpu.get_barrier_semaphore()

    @pl.loop(1, 16)
    def _(k):
        pl.semaphore_signal(barrier, inc=1, device_id=plane(k % 4, k // 4), device_id_type=MESH)

    for device in (partner, far, near):
        pl.semaphore_signal(barrier, inc=1, device_id=device, device_id_type=MESH)
    pl.semaphore_wait(barrier, 18)

    own = pl.ds(0, BLOCK)
    east, west = plane(1, 0), plane(3, 0)
    north, south = plane(0, 1), plane(0, 3)

    def place(b, count=1):
        return pl.ds(BLOCK * b, BLOCK * count)

    a1 = [
        remote(tc.at[:, :, own], tc.at[:, :, place(2)], a_send.at[0], a_recv.at[0], east),
        remote(tc.at[:, :, own], tc.at[:, :, place(1)], a_send.at[1], a_recv.at[1], west),
        remote(tc.at[0, :, place(2)], tc.at[0, :, place(3)], a_send.at[2], a_recv.at[2], east),
        remote(tc.at[1, :, place(1)], tc.at[1, :, place(3)], a_send.at[3], a_recv.at[3], west),
        remote(tc.at[:, :, place(0, 3)], tc.at[:, :, place(12, 3)], a_send.at[4], a_recv.at[4], north),
        remote(tc.at[:, :, place(0, 3)], tc.at[:, :, place(4, 3)], a_send.at[5], a_recv.at[5], south),
        remote(tc.at[:, :, place(3)], tc.at[:, :, place(15)], a_send.at[6], a_recv.at[6], north),
        remote(tc.at[:, :, place(3)], tc.at[:, :, place(7)], a_send.at[7], a_recv.at[7], south),
        remote(tc.at[0, :, place(12, 4)], tc.at[0, :, place(8, 4)], a_send.at[8], a_recv.at[8], north),
        remote(tc.at[1, :, place(4, 4)], tc.at[1, :, place(8, 4)], a_send.at[9], a_recv.at[9], south),
    ]
    weights = [
        remote(wg, wgux.at[0], w_send.at[0], w_recv.at[0], partner),
        remote(wu, wgux.at[1], w_send.at[1], w_recv.at[1], partner),
        remote(wd, wdnx, w_send.at[2], w_recv.at[2], partner),
    ]
    for copy in local[:4]:
        copy.wait()
    a1[0].start()
    a1[1].start()
    for copy in weights:
        copy.start()
    acc[...] = jnp.zeros_like(acc)
    accd[...] = jnp.zeros_like(accd)
    for copy in local[4:]:
        copy.wait()

    def stage_rows(s):
        return pl.ds(pl.multiple_of(s * ROWS, ROWS), ROWS)

    def swap(s):
        return remote(tc.at[:, 1 - core, stage_rows(s)], tx.at[:, stage_rows(s)], x_send.at[s], x_recv.at[s], partner)

    def forward(s):
        swap(s).wait_recv()
        half = s % 2
        mine = tc[:, core, stage_rows(s), :]
        other = tx[:, stage_rows(s), :]
        for t in range(2):
            q[half, :, t * ff : (t + 1) * ff] = jnp.dot(
                mine[0], wgu[t], preferred_element_type=F32
            ) + jnp.dot(other[0], wgux[t], preferred_element_type=F32)
        dims = (((1,), (1,)), ((), ()))
        q[half, :, 2 * ff :] = lax.dot_general(
            mine[1], wdn[...], dims, preferred_element_type=F32
        ) + lax.dot_general(other[1], wdnx[...], dims, preferred_element_type=F32)

    def chunk(o):
        return pl.ds(pl.multiple_of(((o + 16) % 8) * CHUNK, CHUNK), CHUNK)

    def sum_long(s, h):
        return remote(sl.at[s, h - 1], rl.at[s, h - 1], ring_send.at[0], rl_recv.at[s, h - 1], far)

    def sum_short(s, h):
        return remote(ss.at[s, h - 1], rs.at[s, h - 1], ring_send.at[1], rs_recv.at[s, h - 1], near)

    def sum_send(s, h):
        part = q[s % 2, chunk(z + (5 - h) * sign), :]
        if h > 1:
            part = part + rl[s, h - 2].astype(F32)
        sl[s, h - 1] = part.astype(BF16)
        sum_long(s, h).start()
        if h < 4:
            part = q[s % 2, chunk(z - (4 - h) * sign), :]
            if h > 1:
                part = part + rs[s, h - 2].astype(F32)
            ss[s, h - 1] = part.astype(BF16)
            sum_short(s, h).start()

    def sum_wait(s, h):
        sum_long(s, h).wait_recv()
        if h < 4:
            sum_short(s, h).wait_recv()

    def spread_long(s, o, h):
        piece = hid.at[s, core, chunk(o)]
        return remote(piece, piece, ring_send.at[2], al_recv.at[s, h - 1], far)

    def spread_short(s, o, h):
        piece = hid.at[s, core, chunk(o)]
        return remote(piece, piece, ring_send.at[3], as_recv.at[s, h - 1], near)

    def pass_on(s, o):
        piece = hid.at[s, core, chunk(o)]
        remote(piece, piece, pf_send.at[0], pf_recv.at[s], partner).start()

    def spread_send(s, h):
        spread_long(s, z - (h - 1) * sign, h).start()
        if h < 4:
            spread_short(s, z + (h - 1) * sign, h).start()
        pass_on(s, z - (h - 1) * sign)
        if 1 < h:
            pass_on(s, z + (h - 1) * sign)

    def spread_wait(s, h):
        spread_long(s, z - h * sign, h).wait_recv()
        if h < 4:
            spread_short(s, z + h * sign, h).wait_recv()

    def pointwise(s):
        total = q[s % 2, chunk(z), :] + rl[s, 3].astype(F32) + rs[s, 2].astype(F32)
        gate, up, back = total[:, :ff], total[:, ff : 2 * ff], total[:, 2 * ff :]
        sig = jax.nn.sigmoid(gate)
        piece = chunk(z)
        hid[s, core, piece, 0:ff] = (gate * sig * up).astype(BF16)
        hid[s, core, piece, ff : 2 * ff] = (back * up * sig * (1.0 + gate * (1.0 - sig))).astype(BF16)
        hid[s, core, piece, 2 * ff :] = (back * gate * sig).astype(BF16)

    def both_halves(s):
        theirs = hid.at[s, 1 - core]
        return remote(theirs, theirs, pf_send.at[0], pf_recv.at[s], partner)

    def stage_hidden(s, t):
        return hid[s, :, :, t * ff : (t + 1) * ff].reshape(2 * ROWS, ff)

    def stage_tokens(s, t):
        return tc[t, :, stage_rows(s), :].reshape(2 * ROWS, tc.shape[-1])

    def block_copy(k):
        device = plane(shift(k % 4, 4), k // 4)
        return remote(igb.at[:, pl.ds(pl.multiple_of(k * BLOCK, BLOCK), BLOCK)], igr.at[k], ig_send.at[0], ig_recv.at[0], device)

    def input_grad(s):
        both_halves(s).wait_recv()
        dims = (((1,), (1,)), ((), ()))
        block = lax.dot_general(stage_hidden(s, 1), wgu[0], dims, preferred_element_type=F32)
        block = block + lax.dot_general(stage_hidden(s, 2), wgu[1], dims, preferred_element_type=F32)
        igb[:, stage_rows(s), :] = block.astype(BF16).reshape(2, ROWS, block.shape[-1])

        @pl.loop((ROWS * s) // BLOCK, (ROWS * (s + 1)) // BLOCK)
        def _(k):
            @pl.when(k > 0)
            def _():
                block_copy(k).start()

    outer = (((0,), (0,)), ((), ()))

    def column_grads(s):
        left = stage_tokens(s, 0)
        for t in range(2):
            acc[t] += lax.dot_general(left, stage_hidden(s, t + 1), outer, preferred_element_type=F32)

    def down_grad(s):
        accd[...] += lax.dot_general(stage_hidden(s, 0), stage_tokens(s, 1), outer, preferred_element_type=F32)

    a1[0].wait_recv()
    a1[1].wait_recv()
    swap(0).start()
    for n in (2, 3, 4, 5):
        a1[n].start()
    for copy in weights:
        copy.wait_recv()
    forward(0)
    sum_send(0, 1)

    def step(i, carry):
        summing = i < STAGES
        spreading = (i > 0) & (i <= STAGES)
        grads = i > 1

        @pl.when(grads)
        def _():
            input_grad(i - 2)

        def hop(h):
            @pl.when(summing)
            def _():
                sum_wait(i, h - 1)
                sum_send(i, h)

            @pl.when(spreading)
            def _():
                spread_wait(i - 1, h - 1)
                spread_send(i - 1, h)

        hop(2)

        @pl.when(i == 0)
        def _():
            for n in (2, 3):
                a1[n].wait_recv()
            for n in (6, 7):
                a1[n].start()

        @pl.when(i == 1)
        def _():
            for n in (4, 6, 7):
                a1[n].wait_recv()
            for n in (8, 9):
                a1[n].start()

        @pl.when(i == 2)
        def _():
            for n in (8, 9):
                a1[n].wait_recv()

        @pl.when((i > 0) & (i < STAGES - 1))
        def _():
            swap(i + 1).start()

        @pl.when(grads)
        def _():
            column_grads(i - 2)

        hop(3)

        @pl.when(i == 0)
        def _():
            a1[5].wait_recv()
            swap(1).start()

        @pl.when(i < STAGES - 1)
        def _():
            forward(i + 1)

        hop(4)

        @pl.when(i < STAGES - 1)
        def _():
            sum_send(i + 1, 1)

        @pl.when(grads)
        def _():
            down_grad(i - 2)

        @pl.when(summing)
        def _():
            sum_wait(i, 4)
            pointwise(i)
            spread_send(i, 1)

        @pl.when(spreading)
        def _():
            spread_wait(i - 1, 4)
            pass_on(i - 1, z - 4 * sign)

        return carry

    lax.fori_loop(0, STAGES + 2, step, 0)

    gg_out[...] = acc[0].astype(BF16)
    gu_out[...] = acc[1].astype(BF16)
    gd_out[...] = accd[...].astype(BF16)

    arrived = igr.at[pl.ds(1, 15)]
    remote(arrived, arrived, ig_send.at[0], ig_recv.at[0], partner).wait()
    total = igb[:, 0:BLOCK, :].astype(F32)
    for k in range(1, 16):
        total = total + igr[k].astype(F32)
    ig_out[...] = total.reshape(2 * BLOCK, total.shape[-1]).astype(BF16)

    for copy in a1 + weights:
        copy.wait_send()

    @pl.loop(0, STAGES)
    def _(s):
        swap(s).wait_send()

    remote(sl, sl, ring_send.at[0], ring_send.at[0], far).wait_send()
    remote(ss, ss, ring_send.at[1], ring_send.at[1], near).wait_send()
    remote(sl, sl, ring_send.at[2], ring_send.at[2], far).wait_send()
    remote(ss, ss, ring_send.at[3], ring_send.at[3], near).wait_send()
    mine = hid.at[:, core]
    remote(mine, mine, pf_send.at[0], pf_send.at[0], partner).wait_send()


def on_device(tokens, cotangent, gate_weight, up_weight, down_weight):
    width, ff = gate_weight.shape
    DMA = pltpu.SemaphoreType.DMA
    hbm = pl.BlockSpec(memory_space=pl.ANY)
    vmem = pl.BlockSpec(memory_space=pltpu.VMEM)
    return pl.pallas_call(
        kernel,
        out_shape=(
            jax.ShapeDtypeStruct(tokens.shape, BF16),
            jax.ShapeDtypeStruct((width, ff), BF16),
            jax.ShapeDtypeStruct((width, ff), BF16),
            jax.ShapeDtypeStruct((ff, width), BF16),
        ),
        in_specs=[hbm] * 5,
        out_specs=(vmem,) * 4,
        scratch_shapes=[
            pltpu.VMEM((2, 2, HALF, width), BF16),
            pltpu.VMEM((2, HALF, width), BF16),
            pltpu.VMEM((2, width, ff), BF16),
            pltpu.VMEM((ff, width), BF16),
            pltpu.VMEM((2, width, ff), BF16),
            pltpu.VMEM((ff, width), BF16),
            pltpu.VMEM((2, ROWS, 3 * ff), F32),
            pltpu.VMEM((STAGES, 4, CHUNK, 3 * ff), BF16),
            pltpu.VMEM((STAGES, 4, CHUNK, 3 * ff), BF16),
            pltpu.VMEM((STAGES, 3, CHUNK, 3 * ff), BF16),
            pltpu.VMEM((STAGES, 3, CHUNK, 3 * ff), BF16),
            pltpu.VMEM((STAGES, 2, ROWS, 3 * ff), BF16),
            pltpu.VMEM((2, width, ff), F32),
            pltpu.VMEM((ff, width), F32),
            pltpu.VMEM((2, HALF, width), BF16),
            pltpu.VMEM((16, 2, BLOCK, width), BF16),
            DMA((7,)),
            DMA((3,)),
            DMA((3,)),
            DMA((10,)),
            DMA((10,)),
            DMA((STAGES,)),
            DMA((STAGES,)),
            DMA((4,)),
            DMA((STAGES, 4)),
            DMA((STAGES, 3)),
            DMA((STAGES, 4)),
            DMA((STAGES, 3)),
            DMA((1,)),
            DMA((STAGES,)),
            DMA((1,)),
            DMA((1,)),
        ],
        compiler_params=pltpu.CompilerParams(
            collective_id=0, has_side_effects=True, vmem_limit_bytes=60 * 1024 * 1024
        ),
    )(tokens, cotangent, gate_weight, up_weight, down_weight)


def solution(mesh):
    return jax.shard_map(
        on_device,
        mesh=mesh,
        in_specs=(
            P("row", ("depth", "col")),
            P("row", ("depth", "col")),
            P(("depth", "col"), "row"),
            P(("depth", "col"), "row"),
            P("row", ("depth", "col")),
        ),
        out_specs=(
            P("row", ("depth", "col")),
            P(("depth", "col"), "row"),
            P(("depth", "col"), "row"),
            P("row", ("depth", "col")),
        ),
        check_vma=False,
    )
```

```python
import jax
import jax.numpy as jnp
from jax import lax
from jax.experimental import pallas as pl
from jax.experimental.pallas import tpu as pltpu
from jax.sharding import PartitionSpec as P

MESH = pl.DeviceIdType.MESH
BF16 = jnp.bfloat16
F32 = jnp.float32

STAGES = 6
ROWS = 128
CHUNK = 16
BLOCK = 48
HALF = STAGES * ROWS
PARTS = ((0, 1280), (1280, 1408))


PLACES = (
    (0, 0), (1, 0), (0, 1), (2, 0), (3, 1), (3, 3), (1, 3), (2, 1),
    (2, 3), (0, 2), (1, 2), (3, 2), (2, 2), (1, 1), (3, 0), (0, 3),
)


def kernel(
    tok, cot, wg, wu, wd,
    ig_out, gg_out, gu_out, gd_out,
    tc, tx, wgu, wdn, wgux, wdnx, q, sl, rl, ss, rs, hid, igb, igr,
    loc_sem, w_send, w_recv, a_send, a_recv, x_send, x_recv,
    ring_send, rl_recv, rs_recv, al_recv, as_recv, pf_send, pf_recv, ig_send, ig_recv,
):
    ff = wg.shape[1]
    depth, row, col = lax.axis_index("depth"), lax.axis_index("row"), lax.axis_index("col")
    x, y = row // 4, row % 4
    z, core = depth * 2 + col // 2, col % 2
    sign = 1 - 2 * core

    def at(xx, yy, zz, cc):
        return (zz // 2, xx * 4 + yy, (zz % 2) * 2 + cc)

    def plane(dx, dy):
        return at((x + dx) % 4, (y + dy) % 4, z, core)

    partner = at(x, y, z, 1 - core)
    far = at(x, y, (z + sign + 8) % 8, core)
    near = at(x, y, (z - sign + 8) % 8, core)

    def remote(src, dst, send, recv, device):
        return pltpu.make_async_remote_copy(
            src_ref=src, dst_ref=dst, send_sem=send, recv_sem=recv,
            device_id=device, device_id_type=MESH,
        )

    local = [
        pltpu.make_async_copy(src.at[pl.ds(BLOCK * half, BLOCK)], tc.at[t, half, pl.ds(0, BLOCK)], loc_sem.at[2 * t + half])
        for t, src in enumerate((tok, cot))
        for half in range(2)
    ]
    local += [
        pltpu.make_async_copy(wg, wgu.at[0], loc_sem.at[4]),
        pltpu.make_async_copy(wu, wgu.at[1], loc_sem.at[5]),
        pltpu.make_async_copy(wd, wdn, loc_sem.at[6]),
    ]
    for copy in local:
        copy.start()
    barrier = pltpu.get_barrier_semaphore()

    @pl.loop(1, 16)
    def _(k):
        pl.semaphore_signal(barrier, inc=1, device_id=plane(k % 4, k // 4), device_id_type=MESH)

    for device in (partner, far, near):
        pl.semaphore_signal(barrier, inc=1, device_id=device, device_id_type=MESH)
    pl.semaphore_wait(barrier, 18)

    east, west = plane(1, 0), plane(3, 0)
    north, south = plane(0, 1), plane(0, 3)

    def block(t, k):
        rows = pl.ds(BLOCK * k, BLOCK)
        return tc.at[:, :, rows] if t is None else tc.at[t, :, rows]

    hops = (
        (None, 0, 14, east), (None, 0, 1, west), (None, 0, 15, north), (None, 0, 2, south),
        (0, 14, 3, east), (1, 1, 3, west),
        (None, 1, 6, north), (None, 14, 5, north), (None, 14, 4, south), (None, 1, 13, south),
        (0, 15, 9, north), (1, 2, 9, south),
        (None, 3, 8, north), (None, 3, 7, south),
        (0, 6, 10, north), (1, 13, 10, south), (0, 5, 11, north), (1, 4, 11, south),
        (0, 8, 12, north), (1, 7, 12, south),
    )
    a1 = [
        remote(block(t, src), block(t, dst), a_send.at[n], a_recv.at[n], device)
        for n, (t, src, dst, device) in enumerate(hops)
    ]

    def tokens_in(*numbers):
        for n in numbers:
            a1[n].wait_recv()

    def tokens_out(*numbers):
        for n in numbers:
            a1[n].start()

    weights = [
        remote(wg, wgux.at[0], w_send.at[0], w_recv.at[0], partner),
        remote(wu, wgux.at[1], w_send.at[1], w_recv.at[1], partner),
        remote(wd, wdnx, w_send.at[2], w_recv.at[2], partner),
    ]
    for copy in local[:4]:
        copy.wait()
    tokens_out(0, 1, 2, 3)
    for copy in weights:
        copy.start()
    for out in (gg_out, gu_out, gd_out):
        out[...] = jnp.zeros_like(out)
    for copy in local[4:]:
        copy.wait()

    def stage_rows(s):
        return pl.ds(pl.multiple_of(s * ROWS, ROWS), ROWS)

    def swap(s):
        return remote(tc.at[:, 1 - core, stage_rows(s)], tx.at[:, stage_rows(s)], x_send.at[s], x_recv.at[s], partner)

    def forward(s):
        swap(s).wait_recv()
        slot = s % 3
        mine = tc[:, core, stage_rows(s), :]
        other = tx[:, stage_rows(s), :]
        for t in range(2):
            q[slot, :, t * ff : (t + 1) * ff] = jnp.dot(
                mine[0], wgu[t], preferred_element_type=F32
            ) + jnp.dot(other[0], wgux[t], preferred_element_type=F32)
        dims = (((1,), (1,)), ((), ()))
        q[slot, :, 2 * ff :] = lax.dot_general(
            mine[1], wdn[...], dims, preferred_element_type=F32
        ) + lax.dot_general(other[1], wdnx[...], dims, preferred_element_type=F32)

    def chunk(o):
        return pl.ds(pl.multiple_of(((o + 16) % 8) * CHUNK, CHUNK), CHUNK)

    def part_of(ref, p):
        return ref.at[:, pl.ds(*PARTS[p])]

    def sum_long(s, h, p):
        return remote(
            part_of(sl.at[s, h - 1], p), part_of(rl.at[s, h - 1], p), ring_send.at[0], rl_recv.at[s, h - 1, p], far
        )

    def sum_short(s, h, p):
        return remote(
            part_of(ss.at[s, h - 1], p), part_of(rs.at[s, h - 1], p), ring_send.at[1], rs_recv.at[s, h - 1, p], near
        )

    def sum_send(s, h, p):
        cols = pl.ds(*PARTS[p])
        part = q[s % 3, chunk(z + (5 - h) * sign), cols]
        if h > 1:
            part = part + rl[s, h - 2, :, cols].astype(F32)
        sl[s, h - 1, :, cols] = part.astype(BF16)
        sum_long(s, h, p).start()
        if h < 4:
            part = q[s % 3, chunk(z - (4 - h) * sign), cols]
            if h > 1:
                part = part + rs[s, h - 2, :, cols].astype(F32)
            ss[s, h - 1, :, cols] = part.astype(BF16)
            sum_short(s, h, p).start()

    def sum_wait(s, h, p):
        sum_long(s, h, p).wait_recv()
        if h < 4:
            sum_short(s, h, p).wait_recv()

    def sum_on(s, h):
        for p in range(2):
            sum_wait(s, h, p)
            sum_send(s, h + 1, p)

    def piece_of(s, o):
        return hid.at[s, core, chunk(o)]

    def spread_long(s, o, h, p):
        piece = part_of(piece_of(s, o), p)
        return remote(piece, piece, ring_send.at[2], al_recv.at[s, h - 1, p], far)

    def spread_short(s, o, h, p):
        piece = part_of(piece_of(s, o), p)
        return remote(piece, piece, ring_send.at[3], as_recv.at[s, h - 1, p], near)

    def pass_on(s, o):
        piece = piece_of(s, o)
        remote(piece, piece, pf_send.at[0], pf_recv.at[s], partner).start()

    def spread_send(s, h, p):
        spread_long(s, z - (h - 1) * sign, h, p).start()
        if h < 4:
            spread_short(s, z + (h - 1) * sign, h, p).start()

    def spread_wait(s, h, p):
        spread_long(s, z - h * sign, h, p).wait_recv()
        if h < 4:
            spread_short(s, z + h * sign, h, p).wait_recv()

    def spread_on(s, h):
        for p in range(2):
            spread_wait(s, h, p)
            if h < 4:
                spread_send(s, h + 1, p)
        pass_on(s, z - h * sign)
        if h < 4:
            pass_on(s, z + h * sign)

    def pointwise(s):
        total = q[s % 3, chunk(z), :] + rl[s, 3].astype(F32) + rs[s, 2].astype(F32)
        gate, up, back = total[:, :ff], total[:, ff : 2 * ff], total[:, 2 * ff :]
        sig = jax.nn.sigmoid(gate)
        piece = chunk(z)
        hid[s, core, piece, 0:ff] = (gate * sig * up).astype(BF16)
        hid[s, core, piece, ff : 2 * ff] = (back * up * sig * (1.0 + gate * (1.0 - sig))).astype(BF16)
        hid[s, core, piece, 2 * ff :] = (back * gate * sig).astype(BF16)

    def both_halves(s):
        theirs = hid.at[s, 1 - core]
        return remote(theirs, theirs, pf_send.at[0], pf_recv.at[s], partner)

    def stage_hidden(s, t):
        return hid[s, :, :, t * ff : (t + 1) * ff].reshape(2 * ROWS, ff)

    def stage_tokens(s, t):
        return tc[t, :, stage_rows(s), :].reshape(2 * ROWS, tc.shape[-1])

    def block_copy(k):
        return remote(igb.at[:, pl.ds(BLOCK * k, BLOCK)], igr.at[k], ig_send.at[0], ig_recv.at[0], plane(*PLACES[k]))

    def input_grad(s):
        both_halves(s).wait_recv()
        dims = (((1,), (1,)), ((), ()))
        block = lax.dot_general(stage_hidden(s, 1), wgu[0], dims, preferred_element_type=F32)
        block = block + lax.dot_general(stage_hidden(s, 2), wgu[1], dims, preferred_element_type=F32)
        igb[:, stage_rows(s), :] = block.astype(BF16).reshape(2, ROWS, block.shape[-1])

        for stage in range(STAGES):

            @pl.when(s == stage)
            def _():
                for k in range(max(1, ROWS * stage // BLOCK), ROWS * (stage + 1) // BLOCK):
                    block_copy(k).start()

    outer = (((0,), (0,)), ((), ()))

    def column_grads(s):
        left = stage_tokens(s, 0)
        for t, out in enumerate((gg_out, gu_out)):
            out[...] += lax.dot_general(left, stage_hidden(s, t + 1), outer, preferred_element_type=F32)

    def down_grad(s):
        gd_out[...] += lax.dot_general(stage_hidden(s, 0), stage_tokens(s, 1), outer, preferred_element_type=F32)

    tokens_in(0, 1, 2, 3)
    swap(0).start()
    tokens_out(4, 5, 7, 8, 6)
    for copy in weights:
        copy.wait_recv()
    forward(0)
    sum_send(0, 1, 0)
    sum_send(0, 1, 1)

    def step(i, carry):
        front = i < STAGES
        back = (i > 0) & (i < STAGES + 1)
        out_front = (i > 1) & (i < STAGES + 2)
        out_back = (i > 2) & (i < STAGES + 3)
        grads = i > 3
        more = i < STAGES - 1

        @pl.when(back)
        def _():
            sum_on(i - 1, 2)

        @pl.when(out_back)
        def _():
            spread_on(i - 3, 2)

        @pl.when(grads)
        def _():
            input_grad(i - 4)

        @pl.when(front)
        def _():
            sum_on(i, 1)

        @pl.when(out_front)
        def _():
            spread_on(i - 2, 1)

        @pl.when(back)
        def _():
            sum_on(i - 1, 3)

        @pl.when(out_back)
        def _():
            spread_on(i - 3, 3)

        @pl.when(i == 0)
        def _():
            tokens_in(4, 5)
            tokens_out(12, 13, 9, 10, 11)
            tokens_in(7, 8)

        @pl.when(i == 1)
        def _():
            tokens_in(6, 9)
            tokens_out(14, 15, 16, 17)
            tokens_in(12, 13)
            tokens_out(18, 19)

        @pl.when(i == 2)
        def _():
            tokens_in(10, 11, 14, 15)

        @pl.when(i == 3)
        def _():
            tokens_in(16, 17, 18, 19)

        @pl.when(more)
        def _():
            swap(i + 1).start()

        @pl.when(grads)
        def _():
            column_grads(i - 4)

        @pl.when(more)
        def _():
            forward(i + 1)
            sum_send(i + 1, 1, 0)
            sum_send(i + 1, 1, 1)

        @pl.when(back)
        def _():
            sum_wait(i - 1, 4, 0)
            sum_wait(i - 1, 4, 1)
            pointwise(i - 1)
            spread_send(i - 1, 1, 0)
            spread_send(i - 1, 1, 1)
            pass_on(i - 1, z)

        @pl.when(out_back)
        def _():
            spread_on(i - 3, 4)

        @pl.when(grads)
        def _():
            down_grad(i - 4)

        return carry

    lax.fori_loop(0, STAGES + 4, step, 0)

    arrived = igr.at[pl.ds(1, 15)]
    remote(arrived, arrived, ig_send.at[0], ig_recv.at[0], partner).wait()
    total = igb[:, 0:BLOCK, :].astype(F32)
    for k in range(1, 16):
        total = total + igr[k].astype(F32)
    ig_out[...] = total.reshape(2 * BLOCK, total.shape[-1])

    for copy in a1 + weights:
        copy.wait_send()

    @pl.loop(0, STAGES)
    def _(s):
        swap(s).wait_send()

    remote(sl, sl, ring_send.at[0], ring_send.at[0], far).wait_send()
    remote(ss, ss, ring_send.at[1], ring_send.at[1], near).wait_send()
    remote(sl, sl, ring_send.at[2], ring_send.at[2], far).wait_send()
    remote(ss, ss, ring_send.at[3], ring_send.at[3], near).wait_send()
    mine = hid.at[:, core]
    remote(mine, mine, pf_send.at[0], pf_send.at[0], partner).wait_send()


def rounded(*refs):
    wide, out, narrow, sems = refs[:4], refs[4:8], refs[8:12], refs[12]
    copies = [pltpu.make_async_copy(b, o, sems.at[n]) for n, (b, o) in enumerate(zip(narrow, out))]
    for a, b, copy in zip(wide, narrow, copies):
        b[...] = a[...].astype(BF16)
        copy.start()
    for copy in copies:
        copy.wait()


def on_device(tokens, cotangent, gate_weight, up_weight, down_weight):
    width, ff = gate_weight.shape
    DMA = pltpu.SemaphoreType.DMA
    hbm = pl.BlockSpec(memory_space=pltpu.HBM)
    vmem = pl.BlockSpec(memory_space=pltpu.VMEM)
    outs = pl.pallas_call(
        kernel,
        out_shape=(
            pltpu.VMEM(tokens.shape, F32),
            pltpu.VMEM((width, ff), F32),
            pltpu.VMEM((width, ff), F32),
            pltpu.VMEM((ff, width), F32),
        ),
        in_specs=[hbm] * 5,
        out_specs=(vmem,) * 4,
        scratch_shapes=[
            pltpu.VMEM((2, 2, HALF, width), BF16),
            pltpu.VMEM((2, HALF, width), BF16),
            pltpu.VMEM((2, width, ff), BF16),
            pltpu.VMEM((ff, width), BF16),
            pltpu.VMEM((2, width, ff), BF16),
            pltpu.VMEM((ff, width), BF16),
            pltpu.VMEM((3, ROWS, 3 * ff), F32),
            pltpu.VMEM((STAGES, 4, CHUNK, 3 * ff), BF16),
            pltpu.VMEM((STAGES, 4, CHUNK, 3 * ff), BF16),
            pltpu.VMEM((STAGES, 3, CHUNK, 3 * ff), BF16),
            pltpu.VMEM((STAGES, 3, CHUNK, 3 * ff), BF16),
            pltpu.VMEM((STAGES, 2, ROWS, 3 * ff), BF16),
            pltpu.VMEM((2, HALF, width), BF16),
            pltpu.VMEM((16, 2, BLOCK, width), BF16),
            DMA((7,)),
            DMA((3,)),
            DMA((3,)),
            DMA((20,)),
            DMA((20,)),
            DMA((STAGES,)),
            DMA((STAGES,)),
            DMA((4,)),
            DMA((STAGES, 4, 2)),
            DMA((STAGES, 3, 2)),
            DMA((STAGES, 4, 2)),
            DMA((STAGES, 3, 2)),
            DMA((1,)),
            DMA((STAGES,)),
            DMA((1,)),
            DMA((1,)),
        ],
        compiler_params=pltpu.CompilerParams(
            collective_id=0, has_side_effects=True, vmem_limit_bytes=61300000
        ),
    )(tokens, cotangent, gate_weight, up_weight, down_weight)
    outs = [pltpu.with_memory_space_constraint(out, pltpu.VMEM) for out in outs]
    return pl.pallas_call(
        rounded,
        out_shape=tuple(jax.ShapeDtypeStruct(out.shape, BF16) for out in outs),
        in_specs=[vmem] * 4,
        out_specs=(hbm,) * 4,
        scratch_shapes=[pltpu.VMEM(out.shape, BF16) for out in outs] + [DMA((4,))],
        compiler_params=pltpu.CompilerParams(vmem_limit_bytes=16 * 1024 * 1024),
    )(*outs)


def solution(mesh):
    return jax.shard_map(
        on_device,
        mesh=mesh,
        in_specs=(
            P("row", ("depth", "col")),
            P("row", ("depth", "col")),
            P(("depth", "col"), "row"),
            P(("depth", "col"), "row"),
            P("row", ("depth", "col")),
        ),
        out_specs=(
            P("row", ("depth", "col")),
            P(("depth", "col"), "row"),
            P(("depth", "col"), "row"),
            P("row", ("depth", "col")),
        ),
        check_vma=False,
    )
```

```python
import jax
import jax.numpy as jnp
from jax import lax
from jax.experimental import pallas as pl
from jax.experimental.pallas import tpu as pltpu
from jax.sharding import PartitionSpec as P

MESH = pl.DeviceIdType.MESH
BF16 = jnp.bfloat16
F32 = jnp.float32

STAGES = 6
ROWS = 128
CHUNK = 16
BLOCK = 48
HALF = STAGES * ROWS
PARTS = ((0, 1280), (1280, 1408))


PLACES = (
    (0, 0), (1, 0), (0, 1), (2, 0), (3, 1), (3, 3), (1, 3), (2, 1),
    (2, 3), (0, 2), (1, 2), (3, 2), (2, 2), (1, 1), (3, 0), (0, 3),
)


def kernel(
    tok, cot, wg, wu, wd,
    ig_out, gg_out, gu_out, gd_out,
    tc, tx, wgu, wdn, wgux, wdnx, q, sl, rl, ss, rs, hid, igb, igr,
    loc_sem, w_send, w_recv, a_send, a_recv, x_send, x_recv,
    ring_send, rl_recv, rs_recv, al_recv, as_recv, pf_send, pf_recv, ig_send, ig_recv,
):
    ff = wg.shape[1]
    depth, row, col = lax.axis_index("depth"), lax.axis_index("row"), lax.axis_index("col")
    x, y = row // 4, row % 4
    z, core = depth * 2 + col // 2, col % 2
    sign = 1 - 2 * core

    def at(xx, yy, zz, cc):
        return (zz // 2, xx * 4 + yy, (zz % 2) * 2 + cc)

    def plane(dx, dy):
        return at((x + dx) % 4, (y + dy) % 4, z, core)

    partner = at(x, y, z, 1 - core)
    far = at(x, y, (z + sign + 8) % 8, core)
    near = at(x, y, (z - sign + 8) % 8, core)

    def remote(src, dst, send, recv, device):
        return pltpu.make_async_remote_copy(
            src_ref=src, dst_ref=dst, send_sem=send, recv_sem=recv,
            device_id=device, device_id_type=MESH,
        )

    local = [
        pltpu.make_async_copy(src.at[pl.ds(BLOCK * half, BLOCK)], tc.at[t, half, pl.ds(0, BLOCK)], loc_sem.at[2 * t + half])
        for t, src in enumerate((tok, cot))
        for half in range(2)
    ]
    local += [
        pltpu.make_async_copy(wg, wgu.at[0], loc_sem.at[4]),
        pltpu.make_async_copy(wu, wgu.at[1], loc_sem.at[5]),
        pltpu.make_async_copy(wd, wdn, loc_sem.at[6]),
    ]
    for copy in local:
        copy.start()
    barrier = pltpu.get_barrier_semaphore()

    neighbours = (partner, far, near, plane(1, 0), plane(3, 0), plane(0, 1), plane(0, 3))
    for device in neighbours:
        pl.semaphore_signal(barrier, inc=1, device_id=device, device_id_type=MESH)
    pl.semaphore_wait(barrier, len(neighbours))

    east, west = plane(1, 0), plane(3, 0)
    north, south = plane(0, 1), plane(0, 3)

    def block(t, k):
        rows = pl.ds(BLOCK * k, BLOCK)
        return tc.at[:, :, rows] if t is None else tc.at[t, :, rows]

    hops = (
        (None, 0, 14, east), (None, 0, 1, west), (None, 0, 15, north), (None, 0, 2, south),
        (0, 14, 3, east), (1, 1, 3, west),
        (None, 1, 6, north), (None, 14, 5, north), (None, 14, 4, south), (None, 1, 13, south),
        (0, 15, 9, north), (1, 2, 9, south),
        (None, 3, 8, north), (None, 3, 7, south),
        (0, 6, 10, north), (1, 13, 10, south), (0, 5, 11, north), (1, 4, 11, south),
        (0, 8, 12, north), (1, 7, 12, south),
    )
    a1 = [
        remote(block(t, src), block(t, dst), a_send.at[n], a_recv.at[n], device)
        for n, (t, src, dst, device) in enumerate(hops)
    ]

    def tokens_in(*numbers):
        for n in numbers:
            a1[n].wait_recv()

    def tokens_out(*numbers):
        for n in numbers:
            a1[n].start()

    weights = [
        remote(wg, wgux.at[0], w_send.at[0], w_recv.at[0], partner),
        remote(wu, wgux.at[1], w_send.at[1], w_recv.at[1], partner),
        remote(wd, wdnx, w_send.at[2], w_recv.at[2], partner),
    ]
    for copy in local[:4]:
        copy.wait()
    tokens_out(0, 1, 2, 3)
    for copy in weights:
        copy.start()
    for out in (gg_out, gu_out, gd_out):
        out[...] = jnp.zeros_like(out)
    for copy in local[4:]:
        copy.wait()

    def stage_rows(s):
        return pl.ds(pl.multiple_of(s * ROWS, ROWS), ROWS)

    def swap(s):
        return remote(tc.at[:, 1 - core, stage_rows(s)], tx.at[:, stage_rows(s)], x_send.at[s], x_recv.at[s], partner)

    def forward_in(s):
        slot = s % 3
        mine, other = tc[0, core, stage_rows(s), :], tx[0, stage_rows(s), :]
        for t in range(2):
            q[slot, :, t * ff : (t + 1) * ff] = jnp.dot(
                mine, wgu[t], preferred_element_type=F32
            ) + jnp.dot(other, wgux[t], preferred_element_type=F32)

    def forward_out(s):
        slot = s % 3
        mine, other = tc[1, core, stage_rows(s), :], tx[1, stage_rows(s), :]
        dims = (((1,), (1,)), ((), ()))
        q[slot, :, 2 * ff :] = lax.dot_general(
            mine, wdn[...], dims, preferred_element_type=F32
        ) + lax.dot_general(other, wdnx[...], dims, preferred_element_type=F32)

    def chunk(o):
        return pl.ds(pl.multiple_of(((o + 16) % 8) * CHUNK, CHUNK), CHUNK)

    def part_of(ref, p):
        return ref.at[:, pl.ds(*PARTS[p])]

    def sum_long(s, h, p):
        return remote(
            part_of(sl.at[s, h - 1], p), part_of(rl.at[s, h - 1], p), ring_send.at[0], rl_recv.at[s, h - 1, p], far
        )

    def sum_short(s, h, p):
        return remote(
            part_of(ss.at[s, h - 1], p), part_of(rs.at[s, h - 1], p), ring_send.at[1], rs_recv.at[s, h - 1, p], near
        )

    def sum_send(s, h, p):
        cols = pl.ds(*PARTS[p])
        part = q[s % 3, chunk(z + (5 - h) * sign), cols]
        if h > 1:
            part = part + rl[s, h - 2, :, cols].astype(F32)
        sl[s, h - 1, :, cols] = part.astype(BF16)
        sum_long(s, h, p).start()
        if h < 4:
            part = q[s % 3, chunk(z - (4 - h) * sign), cols]
            if h > 1:
                part = part + rs[s, h - 2, :, cols].astype(F32)
            ss[s, h - 1, :, cols] = part.astype(BF16)
            sum_short(s, h, p).start()

    def sum_wait(s, h, p):
        sum_long(s, h, p).wait_recv()
        if h < 4:
            sum_short(s, h, p).wait_recv()

    def sum_on(s, h):
        for p in range(2):
            sum_wait(s, h, p)
            sum_send(s, h + 1, p)

    def piece_of(s, o):
        return hid.at[s, core, chunk(o)]

    def spread_long(s, o, h, p):
        piece = part_of(piece_of(s, o), p)
        return remote(piece, piece, ring_send.at[2], al_recv.at[s, h - 1, p], far)

    def spread_short(s, o, h, p):
        piece = part_of(piece_of(s, o), p)
        return remote(piece, piece, ring_send.at[3], as_recv.at[s, h - 1, p], near)

    def pass_on(s, o):
        piece = piece_of(s, o)
        remote(piece, piece, pf_send.at[0], pf_recv.at[s], partner).start()

    def spread_send(s, h, p):
        spread_long(s, z - (h - 1) * sign, h, p).start()
        if h < 4:
            spread_short(s, z + (h - 1) * sign, h, p).start()

    def spread_wait(s, h, p):
        spread_long(s, z - h * sign, h, p).wait_recv()
        if h < 4:
            spread_short(s, z + h * sign, h, p).wait_recv()

    def spread_on(s, h):
        for p in range(2):
            spread_wait(s, h, p)
            if h < 4:
                spread_send(s, h + 1, p)
        pass_on(s, z - h * sign)
        if h < 4:
            pass_on(s, z + h * sign)

    def pointwise(s):
        total = q[s % 3, chunk(z), :] + rl[s, 3].astype(F32) + rs[s, 2].astype(F32)
        gate, up, back = total[:, :ff], total[:, ff : 2 * ff], total[:, 2 * ff :]
        sig = jax.nn.sigmoid(gate)
        piece = chunk(z)
        hid[s, core, piece, 0:ff] = (gate * sig * up).astype(BF16)
        hid[s, core, piece, ff : 2 * ff] = (back * up * sig * (1.0 + gate * (1.0 - sig))).astype(BF16)
        hid[s, core, piece, 2 * ff :] = (back * gate * sig).astype(BF16)

    def both_halves(s):
        theirs = hid.at[s, 1 - core]
        return remote(theirs, theirs, pf_send.at[0], pf_recv.at[s], partner)

    def stage_hidden(s, t):
        return hid[s, :, :, t * ff : (t + 1) * ff].reshape(2 * ROWS, ff)

    def stage_tokens(s, t):
        return tc[t, :, stage_rows(s), :].reshape(2 * ROWS, tc.shape[-1])

    def block_copy(k):
        return remote(igb.at[:, pl.ds(BLOCK * k, BLOCK)], igr.at[k], ig_send.at[0], ig_recv.at[0], plane(*PLACES[k]))

    def input_grad(s):
        both_halves(s).wait_recv()
        dims = (((1,), (1,)), ((), ()))
        block = lax.dot_general(stage_hidden(s, 1), wgu[0], dims, preferred_element_type=F32)
        block = block + lax.dot_general(stage_hidden(s, 2), wgu[1], dims, preferred_element_type=F32)
        igb[:, stage_rows(s), :] = block.astype(BF16).reshape(2, ROWS, block.shape[-1])

        for stage in range(STAGES):

            @pl.when(s == stage)
            def _():
                for k in range(max(1, ROWS * stage // BLOCK), ROWS * (stage + 1) // BLOCK):
                    block_copy(k).start()

    outer = (((0,), (0,)), ((), ()))

    def column_grads(s):
        left = stage_tokens(s, 0)
        for t, out in enumerate((gg_out, gu_out)):
            out[...] += lax.dot_general(left, stage_hidden(s, t + 1), outer, preferred_element_type=F32)

    def down_grad(s):
        gd_out[...] += lax.dot_general(stage_hidden(s, 0), stage_tokens(s, 1), outer, preferred_element_type=F32)

    tokens_in(0, 1, 2, 3)
    swap(0).start()
    tokens_out(4, 5, 7, 8, 6, 9)
    for copy in weights[:2]:
        copy.wait_recv()
    swap(0).wait_recv()
    forward_in(0)
    sum_send(0, 1, 0)
    weights[2].wait_recv()
    forward_out(0)
    sum_send(0, 1, 1)

    def step(i, carry):
        front = i < STAGES
        back = (i > 0) & (i < STAGES + 1)
        out_front = (i > 1) & (i < STAGES + 2)
        out_back = (i > 2) & (i < STAGES + 3)
        grads = i > 3
        more = i < STAGES - 1

        @pl.when(i == 0)
        def _():
            tokens_in(4, 5)
            tokens_out(12, 13, 10, 11)
            tokens_in(7, 8)
            swap(1).start()

        @pl.when(back)
        def _():
            sum_on(i - 1, 2)

        @pl.when(out_back)
        def _():
            spread_on(i - 3, 2)

        @pl.when(grads)
        def _():
            input_grad(i - 4)

        @pl.when(front)
        def _():
            sum_on(i, 1)

        @pl.when(out_front)
        def _():
            spread_on(i - 2, 1)

        @pl.when(i == 1)
        def _():
            tokens_in(6, 9)
            tokens_out(14, 15, 16, 17)
            tokens_in(12, 13)
            tokens_out(18, 19)

        @pl.when(i == 2)
        def _():
            tokens_in(10, 11, 14, 15)

        @pl.when(i == 3)
        def _():
            tokens_in(16, 17, 18, 19)

        @pl.when((i > 0) & more)
        def _():
            swap(i + 1).start()

        @pl.when(back)
        def _():
            sum_on(i - 1, 3)

        @pl.when(out_back)
        def _():
            spread_on(i - 3, 3)

        @pl.when(grads)
        def _():
            column_grads(i - 4)

        @pl.when(more)
        def _():
            swap(i + 1).wait_recv()
            forward_in(i + 1)
            sum_send(i + 1, 1, 0)
            forward_out(i + 1)
            sum_send(i + 1, 1, 1)

        @pl.when(back)
        def _():
            sum_wait(i - 1, 4, 0)
            sum_wait(i - 1, 4, 1)
            pointwise(i - 1)
            spread_send(i - 1, 1, 0)
            spread_send(i - 1, 1, 1)
            pass_on(i - 1, z)

        @pl.when(out_back)
        def _():
            spread_on(i - 3, 4)

        @pl.when(grads)
        def _():
            down_grad(i - 4)

        return carry

    lax.fori_loop(0, STAGES + 4, step, 0)

    arrived = igr.at[pl.ds(1, 15)]
    remote(arrived, arrived, ig_send.at[0], ig_recv.at[0], partner).wait()
    total = igb[:, 0:BLOCK, :].astype(F32)
    for k in range(1, 16):
        total = total + igr[k].astype(F32)
    ig_out[...] = total.reshape(2 * BLOCK, total.shape[-1])

    for copy in a1 + weights:
        copy.wait_send()

    @pl.loop(0, STAGES)
    def _(s):
        swap(s).wait_send()

    remote(sl, sl, ring_send.at[0], ring_send.at[0], far).wait_send()
    remote(ss, ss, ring_send.at[1], ring_send.at[1], near).wait_send()
    remote(sl, sl, ring_send.at[2], ring_send.at[2], far).wait_send()
    remote(ss, ss, ring_send.at[3], ring_send.at[3], near).wait_send()
    mine = hid.at[:, core]
    remote(mine, mine, pf_send.at[0], pf_send.at[0], partner).wait_send()


def rounded(*refs):
    wide, out, narrow, sems = refs[:4], refs[4:8], refs[8:12], refs[12]
    copies = [pltpu.make_async_copy(b, o, sems.at[n]) for n, (b, o) in enumerate(zip(narrow, out))]
    for a, b, copy in zip(wide, narrow, copies):
        b[...] = a[...].astype(BF16)
        copy.start()
    for copy in copies:
        copy.wait()


def on_device(tokens, cotangent, gate_weight, up_weight, down_weight):
    width, ff = gate_weight.shape
    DMA = pltpu.SemaphoreType.DMA
    hbm = pl.BlockSpec(memory_space=pltpu.HBM)
    vmem = pl.BlockSpec(memory_space=pltpu.VMEM)
    outs = pl.pallas_call(
        kernel,
        out_shape=(
            pltpu.VMEM(tokens.shape, F32),
            pltpu.VMEM((width, ff), F32),
            pltpu.VMEM((width, ff), F32),
            pltpu.VMEM((ff, width), F32),
        ),
        in_specs=[hbm] * 5,
        out_specs=(vmem,) * 4,
        scratch_shapes=[
            pltpu.VMEM((2, 2, HALF, width), BF16),
            pltpu.VMEM((2, HALF, width), BF16),
            pltpu.VMEM((2, width, ff), BF16),
            pltpu.VMEM((ff, width), BF16),
            pltpu.VMEM((2, width, ff), BF16),
            pltpu.VMEM((ff, width), BF16),
            pltpu.VMEM((3, ROWS, 3 * ff), F32),
            pltpu.VMEM((STAGES, 4, CHUNK, 3 * ff), BF16),
            pltpu.VMEM((STAGES, 4, CHUNK, 3 * ff), BF16),
            pltpu.VMEM((STAGES, 3, CHUNK, 3 * ff), BF16),
            pltpu.VMEM((STAGES, 3, CHUNK, 3 * ff), BF16),
            pltpu.VMEM((STAGES, 2, ROWS, 3 * ff), BF16),
            pltpu.VMEM((2, HALF, width), BF16),
            pltpu.VMEM((16, 2, BLOCK, width), BF16),
            DMA((7,)),
            DMA((3,)),
            DMA((3,)),
            DMA((20,)),
            DMA((20,)),
            DMA((STAGES,)),
            DMA((STAGES,)),
            DMA((4,)),
            DMA((STAGES, 4, 2)),
            DMA((STAGES, 3, 2)),
            DMA((STAGES, 4, 2)),
            DMA((STAGES, 3, 2)),
            DMA((1,)),
            DMA((STAGES,)),
            DMA((1,)),
            DMA((1,)),
        ],
        compiler_params=pltpu.CompilerParams(
            collective_id=0, has_side_effects=True, vmem_limit_bytes=61300000
        ),
    )(tokens, cotangent, gate_weight, up_weight, down_weight)
    outs = [pltpu.with_memory_space_constraint(out, pltpu.VMEM) for out in outs]
    return pl.pallas_call(
        rounded,
        out_shape=tuple(jax.ShapeDtypeStruct(out.shape, BF16) for out in outs),
        in_specs=[vmem] * 4,
        out_specs=(hbm,) * 4,
        scratch_shapes=[pltpu.VMEM(out.shape, BF16) for out in outs] + [DMA((4,))],
        compiler_params=pltpu.CompilerParams(vmem_limit_bytes=16 * 1024 * 1024),
    )(*outs)


def solution(mesh):
    return jax.shard_map(
        on_device,
        mesh=mesh,
        in_specs=(
            P("row", ("depth", "col")),
            P("row", ("depth", "col")),
            P(("depth", "col"), "row"),
            P(("depth", "col"), "row"),
            P("row", ("depth", "col")),
        ),
        out_specs=(
            P("row", ("depth", "col")),
            P(("depth", "col"), "row"),
            P(("depth", "col"), "row"),
            P("row", ("depth", "col")),
        ),
        check_vma=False,
    )
```

```python
import jax
import jax.numpy as jnp
from jax import lax
from jax.experimental import pallas as pl
from jax.experimental.pallas import tpu as pltpu
from jax.sharding import PartitionSpec as P

MESH = pl.DeviceIdType.MESH
BF16 = jnp.bfloat16
F32 = jnp.float32

STAGES = 6
ROWS = 128
CHUNK = 16
BLOCK = 48
HALF = STAGES * ROWS
LATE = (STAGES - 1) * ROWS // BLOCK
PARTS = ((0, 1280), (1280, 1408))


PLACES = (
    (0, 0), (1, 0), (0, 1), (2, 0), (3, 1), (3, 3), (1, 3), (2, 1),
    (2, 3), (0, 2), (1, 2), (3, 2), (2, 2), (1, 1), (3, 0), (0, 3),
)


def kernel(
    tok, cot, wg, wu, wd,
    ig_out, gg_out, gu_out, gd_out,
    tc, tx, wgu, wdn, wgux, wdnx, q, sl, rl, ss, rs, hid, accg, accu, accd, igb, igr,
    loc_sem, w_send, w_recv, a_send, a_recv, x_send, x_recv,
    ring_send, rl_recv, rs_recv, al_recv, as_recv, pf_send, pf_recv, ig_send, ig_recv,
):
    ff = wg.shape[1]
    depth, row, col = lax.axis_index("depth"), lax.axis_index("row"), lax.axis_index("col")
    x, y = row // 4, row % 4
    z, core = depth * 2 + col // 2, col % 2
    sign = 1 - 2 * core

    def at(xx, yy, zz, cc):
        return (zz // 2, xx * 4 + yy, (zz % 2) * 2 + cc)

    def plane(dx, dy):
        return at((x + dx) % 4, (y + dy) % 4, z, core)

    partner = at(x, y, z, 1 - core)
    far = at(x, y, (z + sign + 8) % 8, core)
    near = at(x, y, (z - sign + 8) % 8, core)

    def remote(src, dst, send, recv, device):
        return pltpu.make_async_remote_copy(
            src_ref=src, dst_ref=dst, send_sem=send, recv_sem=recv,
            device_id=device, device_id_type=MESH,
        )

    local = [
        pltpu.make_async_copy(src.at[pl.ds(BLOCK * half, BLOCK)], tc.at[t, half, pl.ds(0, BLOCK)], loc_sem.at[2 * t + half])
        for t, src in enumerate((tok, cot))
        for half in range(2)
    ]
    local += [
        pltpu.make_async_copy(wg, wgu.at[0], loc_sem.at[4]),
        pltpu.make_async_copy(wu, wgu.at[1], loc_sem.at[5]),
        pltpu.make_async_copy(wd, wdn, loc_sem.at[6]),
    ]
    for copy in local:
        copy.start()
    barrier = pltpu.get_barrier_semaphore()

    neighbours = (partner, far, near, plane(1, 0), plane(3, 0), plane(0, 1), plane(0, 3))
    for device in neighbours:
        pl.semaphore_signal(barrier, inc=1, device_id=device, device_id_type=MESH)
    pl.semaphore_wait(barrier, len(neighbours))

    east, west = plane(1, 0), plane(3, 0)
    north, south = plane(0, 1), plane(0, 3)

    def block(t, k):
        rows = pl.ds(BLOCK * k, BLOCK)
        return tc.at[:, :, rows] if t is None else tc.at[t, :, rows]

    hops = (
        (0, 0, 14, east), (0, 0, 1, west), (0, 0, 15, north), (0, 0, 2, south),
        (0, 14, 3, east), (1, 1, 3, west),
        (None, 1, 6, north), (None, 14, 5, north), (None, 14, 4, south), (None, 1, 13, south),
        (0, 15, 9, north), (1, 2, 9, south),
        (None, 3, 8, north), (None, 3, 7, south),
        (0, 6, 10, north), (1, 13, 10, south), (0, 5, 11, north), (1, 4, 11, south),
        (0, 8, 12, north), (1, 7, 12, south),
        (1, 0, 14, east), (1, 0, 1, west), (1, 0, 15, north), (1, 0, 2, south),
    )
    a1 = [
        remote(block(t, src), block(t, dst), a_send.at[n], a_recv.at[n], device)
        for n, (t, src, dst, device) in enumerate(hops)
    ]

    def tokens_in(*numbers):
        for n in numbers:
            a1[n].wait_recv()

    def tokens_out(*numbers):
        for n in numbers:
            a1[n].start()

    weights = [
        remote(wg, wgux.at[0], w_send.at[0], w_recv.at[0], partner),
        remote(wu, wgux.at[1], w_send.at[1], w_recv.at[1], partner),
        remote(wd, wdnx, w_send.at[2], w_recv.at[2], partner),
    ]
    for copy in local[:4]:
        copy.wait()
    tokens_out(0, 1, 2, 3, 20, 21, 22, 23)
    for copy in weights:
        copy.start()
    sums = (accg, accu, accd)
    for total in sums:
        total[...] = jnp.zeros_like(total)
    for copy in local[4:]:
        copy.wait()

    def stage_rows(s):
        return pl.ds(pl.multiple_of(s * ROWS, ROWS), ROWS)

    def swap(s, t):
        rows = stage_rows(s)
        return remote(tc.at[t, 1 - core, rows], tx.at[t, rows], x_send.at[s, t], x_recv.at[s, t], partner)

    def forward_in(s):
        swap(s, 0).wait_recv()
        slot = s % 3
        mine, other = tc[0, core, stage_rows(s), :], tx[0, stage_rows(s), :]
        for t in range(2):
            q[slot, :, t * ff : (t + 1) * ff] = jnp.dot(
                mine, wgu[t], preferred_element_type=F32
            ) + jnp.dot(other, wgux[t], preferred_element_type=F32)

    def forward_out(s):
        swap(s, 1).wait_recv()
        slot = s % 3
        mine, other = tc[1, core, stage_rows(s), :], tx[1, stage_rows(s), :]
        dims = (((1,), (1,)), ((), ()))
        q[slot, :, 2 * ff :] = lax.dot_general(
            mine, wdn[...], dims, preferred_element_type=F32
        ) + lax.dot_general(other, wdnx[...], dims, preferred_element_type=F32)

    def chunk(o):
        return pl.ds(pl.multiple_of(((o + 16) % 8) * CHUNK, CHUNK), CHUNK)

    def part_of(ref, p):
        return ref.at[:, pl.ds(*PARTS[p])]

    def sum_long(s, h, p):
        return remote(
            part_of(sl.at[s, h - 1], p), part_of(rl.at[s, h - 1], p), ring_send.at[0], rl_recv.at[s, h - 1, p], far
        )

    def sum_short(s, h, p):
        return remote(
            part_of(ss.at[s, h - 1], p), part_of(rs.at[s, h - 1], p), ring_send.at[1], rs_recv.at[s, h - 1, p], near
        )

    def sum_send(s, h, p):
        cols = pl.ds(*PARTS[p])
        part = q[s % 3, chunk(z + (5 - h) * sign), cols]
        if h > 1:
            part = part + rl[s, h - 2, :, cols].astype(F32)
        sl[s, h - 1, :, cols] = part.astype(BF16)
        sum_long(s, h, p).start()
        if h < 4:
            part = q[s % 3, chunk(z - (4 - h) * sign), cols]
            if h > 1:
                part = part + rs[s, h - 2, :, cols].astype(F32)
            ss[s, h - 1, :, cols] = part.astype(BF16)
            sum_short(s, h, p).start()

    def sum_wait(s, h, p):
        sum_long(s, h, p).wait_recv()
        if h < 4:
            sum_short(s, h, p).wait_recv()

    def sum_on(s, h):
        for p in range(2):
            sum_wait(s, h, p)
            sum_send(s, h + 1, p)

    def piece_of(s, o):
        return hid.at[s, core, chunk(o)]

    def spread_long(s, o, h, p):
        piece = part_of(piece_of(s, o), p)
        return remote(piece, piece, ring_send.at[2], al_recv.at[s, h - 1, p], far)

    def spread_short(s, o, h, p):
        piece = part_of(piece_of(s, o), p)
        return remote(piece, piece, ring_send.at[3], as_recv.at[s, h - 1, p], near)

    def pass_on(s, o):
        piece = piece_of(s, o)
        remote(piece, piece, pf_send.at[0], pf_recv.at[s], partner).start()

    def spread_send(s, h, p):
        spread_long(s, z - (h - 1) * sign, h, p).start()
        if h < 4:
            spread_short(s, z + (h - 1) * sign, h, p).start()

    def spread_wait(s, h, p):
        spread_long(s, z - h * sign, h, p).wait_recv()
        if h < 4:
            spread_short(s, z + h * sign, h, p).wait_recv()

    def spread_on(s, h):
        for p in range(2):
            spread_wait(s, h, p)
            if h < 4:
                spread_send(s, h + 1, p)
        pass_on(s, z - h * sign)
        if h < 4:
            pass_on(s, z + h * sign)

    def pointwise(s):
        total = q[s % 3, chunk(z), :] + rl[s, 3].astype(F32) + rs[s, 2].astype(F32)
        gate, up, back = total[:, :ff], total[:, ff : 2 * ff], total[:, 2 * ff :]
        sig = jax.nn.sigmoid(gate)
        piece = chunk(z)
        hid[s, core, piece, 0:ff] = (gate * sig * up).astype(BF16)
        hid[s, core, piece, ff : 2 * ff] = (back * up * sig * (1.0 + gate * (1.0 - sig))).astype(BF16)
        hid[s, core, piece, 2 * ff :] = (back * gate * sig).astype(BF16)

    def both_halves(s):
        theirs = hid.at[s, 1 - core]
        return remote(theirs, theirs, pf_send.at[0], pf_recv.at[s], partner)

    def stage_hidden(s, t):
        return hid[s, :, :, t * ff : (t + 1) * ff].reshape(2 * ROWS, ff)

    def stage_tokens(s, t):
        return tc[t, :, stage_rows(s), :].reshape(2 * ROWS, tc.shape[-1])

    def block_copy(k, half):
        rows = pl.ds(BLOCK * k, BLOCK)
        late = k >= LATE
        return remote(igb.at[half, rows], igr.at[k, half], ig_send.at[int(late)], ig_recv.at[int(late)], plane(*PLACES[k]))

    def half_grad(s, half):
        dims = (((1,), (1,)), ((), ()))
        block = lax.dot_general(hid[s, half, :, ff : 2 * ff], wgu[0], dims, preferred_element_type=F32)
        block = block + lax.dot_general(hid[s, half, :, 2 * ff :], wgu[1], dims, preferred_element_type=F32)
        igb[half, stage_rows(s), :] = block.astype(BF16)

        for stage in range(STAGES):

            @pl.when(s == stage)
            def _():
                for k in range(max(1, ROWS * stage // BLOCK), ROWS * (stage + 1) // BLOCK):
                    block_copy(k, half).start()

    def input_grad(s):
        half_grad(s, core)
        both_halves(s).wait_recv()
        half_grad(s, 1 - core)

    outer = (((0,), (0,)), ((), ()))

    def column_grads(s):
        left = stage_tokens(s, 0)
        for t, out in enumerate(sums[:2]):
            out[...] += lax.dot_general(left, stage_hidden(s, t + 1), outer, preferred_element_type=F32)

    def down_grad(s):
        accd[...] += lax.dot_general(stage_hidden(s, 0), stage_tokens(s, 1), outer, preferred_element_type=F32)

    tokens_in(0, 1, 2, 3)
    swap(0, 0).start()
    tokens_out(4)
    for copy in weights[:2]:
        copy.wait_recv()
    forward_in(0)
    sum_send(0, 1, 0)
    tokens_in(20, 21, 22, 23)
    swap(0, 1).start()
    tokens_out(5, 7, 8, 6, 9)
    weights[2].wait_recv()
    forward_out(0)
    sum_send(0, 1, 1)

    def step(i, carry):
        front = i < STAGES
        back = (i > 0) & (i < STAGES + 1)
        out_front = (i > 1) & (i < STAGES + 2)
        out_back = (i > 2) & (i < STAGES + 3)
        grads = i > 3
        more = i < STAGES - 1

        @pl.when(i == 0)
        def _():
            tokens_in(4, 5)
            tokens_out(12, 13, 10, 11)
            tokens_in(7, 8)
            swap(1, 0).start()
            swap(1, 1).start()

        @pl.when(back)
        def _():
            sum_on(i - 1, 2)

        @pl.when(out_back)
        def _():
            spread_on(i - 3, 2)

        @pl.when(grads)
        def _():
            input_grad(i - 4)

        @pl.when(front)
        def _():
            sum_on(i, 1)

        @pl.when(grads)
        def _():
            down_grad(i - 4)

        @pl.when(i == 1)
        def _():
            tokens_in(6, 9)
            tokens_out(14, 15, 16, 17)
            tokens_in(12, 13)
            tokens_out(18, 19)

        @pl.when(i == 2)
        def _():
            tokens_in(10, 11, 14, 15)

        @pl.when(i == 3)
        def _():
            tokens_in(16, 17, 18, 19)

        @pl.when((i > 0) & more)
        def _():
            swap(i + 1, 0).start()
            swap(i + 1, 1).start()

        @pl.when(back)
        def _():
            sum_on(i - 1, 3)

        @pl.when(out_front)
        def _():
            spread_on(i - 2, 1)

        @pl.when(out_back)
        def _():
            spread_on(i - 3, 3)

        @pl.when(grads)
        def _():
            column_grads(i - 4)

        @pl.when(more)
        def _():
            forward_in(i + 1)
            sum_send(i + 1, 1, 0)
            forward_out(i + 1)
            sum_send(i + 1, 1, 1)

        @pl.when(back)
        def _():
            sum_wait(i - 1, 4, 0)
            sum_wait(i - 1, 4, 1)
            pointwise(i - 1)
            spread_send(i - 1, 1, 0)
            spread_send(i - 1, 1, 1)
            pass_on(i - 1, z)

        @pl.when(out_back)
        def _():
            spread_on(i - 3, 4)

        return carry

    lax.fori_loop(0, STAGES + 4, step, 0)

    for out, total in zip((gg_out, gu_out, gd_out), sums):
        out[...] = total[...].astype(BF16)

    def arrived(first, last, late):
        blocks = igr.at[pl.ds(first, last - first)]
        remote(blocks, blocks, ig_send.at[late], ig_recv.at[late], partner).wait()

    arrived(1, LATE, 0)
    total = igb[:, 0:BLOCK, :].astype(F32)
    for k in range(1, LATE):
        total = total + igr[k].astype(F32)
    arrived(LATE, 16, 1)
    for k in range(LATE, 16):
        total = total + igr[k].astype(F32)
    ig_out[...] = total.reshape(2 * BLOCK, total.shape[-1]).astype(BF16)

    for copy in a1 + weights:
        copy.wait_send()

    @pl.loop(0, STAGES)
    def _(s):
        swap(s, 0).wait_send()
        swap(s, 1).wait_send()

    remote(sl, sl, ring_send.at[0], ring_send.at[0], far).wait_send()
    remote(ss, ss, ring_send.at[1], ring_send.at[1], near).wait_send()
    remote(sl, sl, ring_send.at[2], ring_send.at[2], far).wait_send()
    remote(ss, ss, ring_send.at[3], ring_send.at[3], near).wait_send()
    mine = hid.at[:, core]
    remote(mine, mine, pf_send.at[0], pf_send.at[0], partner).wait_send()


def stored(*refs):
    copies = [pltpu.make_async_copy(refs[n], refs[4 + n], refs[8].at[n]) for n in range(4)]
    for copy in copies:
        copy.start()
    for copy in copies:
        copy.wait()


def on_device(tokens, cotangent, gate_weight, up_weight, down_weight):
    width, ff = gate_weight.shape
    DMA = pltpu.SemaphoreType.DMA
    hbm = pl.BlockSpec(memory_space=pltpu.HBM)
    vmem = pl.BlockSpec(memory_space=pltpu.VMEM)
    outs = pl.pallas_call(
        kernel,
        out_shape=(
            pltpu.VMEM(tokens.shape, BF16),
            pltpu.VMEM((width, ff), BF16),
            pltpu.VMEM((width, ff), BF16),
            pltpu.VMEM((ff, width), BF16),
        ),
        in_specs=[hbm] * 5,
        out_specs=(vmem,) * 4,
        scratch_shapes=[
            pltpu.VMEM((2, 2, HALF, width), BF16),
            pltpu.VMEM((2, HALF, width), BF16),
            pltpu.VMEM((2, width, ff), BF16),
            pltpu.VMEM((ff, width), BF16),
            pltpu.VMEM((2, width, ff), BF16),
            pltpu.VMEM((ff, width), BF16),
            pltpu.VMEM((3, ROWS, 3 * ff), F32),
            pltpu.VMEM((STAGES, 4, CHUNK, 3 * ff), BF16),
            pltpu.VMEM((STAGES, 4, CHUNK, 3 * ff), BF16),
            pltpu.VMEM((STAGES, 3, CHUNK, 3 * ff), BF16),
            pltpu.VMEM((STAGES, 3, CHUNK, 3 * ff), BF16),
            pltpu.VMEM((STAGES, 2, ROWS, 3 * ff), BF16),
            pltpu.VMEM((width, ff), F32),
            pltpu.VMEM((width, ff), F32),
            pltpu.VMEM((ff, width), F32),
            pltpu.VMEM((2, HALF, width), BF16),
            pltpu.VMEM((16, 2, BLOCK, width), BF16),
            DMA((7,)),
            DMA((3,)),
            DMA((3,)),
            DMA((24,)),
            DMA((24,)),
            DMA((STAGES, 2)),
            DMA((STAGES, 2)),
            DMA((4,)),
            DMA((STAGES, 4, 2)),
            DMA((STAGES, 3, 2)),
            DMA((STAGES, 4, 2)),
            DMA((STAGES, 3, 2)),
            DMA((1,)),
            DMA((STAGES,)),
            DMA((2,)),
            DMA((2,)),
        ],
        compiler_params=pltpu.CompilerParams(
            collective_id=0, has_side_effects=True, vmem_limit_bytes=64150000
        ),
    )(tokens, cotangent, gate_weight, up_weight, down_weight)
    outs = [pltpu.with_memory_space_constraint(out, pltpu.VMEM) for out in outs]
    return pl.pallas_call(
        stored,
        out_shape=tuple(jax.ShapeDtypeStruct(out.shape, BF16) for out in outs),
        in_specs=[vmem] * 4,
        out_specs=(hbm,) * 4,
        scratch_shapes=[DMA((4,))],
        compiler_params=pltpu.CompilerParams(vmem_limit_bytes=1024 * 1024),
    )(*outs)


def solution(mesh):
    return jax.shard_map(
        on_device,
        mesh=mesh,
        in_specs=(
            P("row", ("depth", "col")),
            P("row", ("depth", "col")),
            P(("depth", "col"), "row"),
            P(("depth", "col"), "row"),
            P("row", ("depth", "col")),
        ),
        out_specs=(
            P("row", ("depth", "col")),
            P(("depth", "col"), "row"),
            P(("depth", "col"), "row"),
            P("row", ("depth", "col")),
        ),
        check_vma=False,
    )
```

```python
import jax
import jax.numpy as jnp
from jax import lax
from jax.experimental import pallas as pl
from jax.experimental.pallas import tpu as pltpu
from jax.sharding import PartitionSpec as P

MESH = pl.DeviceIdType.MESH
BF16 = jnp.bfloat16
F32 = jnp.float32

STAGES = 6
ROWS = 128
CHUNK = 16
BLOCK = 48
HALF = STAGES * ROWS
LATE = (STAGES - 1) * ROWS // BLOCK
PARTS = ((0, 1280), (1280, 1408))


PLACES = (
    (0, 0), (1, 0), (0, 1), (2, 0), (3, 1), (3, 3), (1, 3), (2, 1),
    (2, 3), (0, 2), (1, 2), (3, 2), (2, 2), (1, 1), (3, 0), (0, 3),
)


def kernel(
    tok, cot, wg, wu, wd,
    ig_out, gg_out, gu_out, gd_out,
    tc, tx, wgu, wdn, wgux, wdnx, q, sl, rl, ss, rs, hid, accg, accu, accd, igb, igr,
    loc_sem, w_send, w_recv, a_send, a_recv, x_send, x_recv,
    ring_send, rl_recv, rs_recv, al_recv, as_recv, pf_send, pf_recv, ig_send, ig_recv,
):
    ff = wg.shape[1]
    depth, row, col = lax.axis_index("depth"), lax.axis_index("row"), lax.axis_index("col")
    x, y = row // 4, row % 4
    z, core = depth * 2 + col // 2, col % 2
    sign = 1 - 2 * core

    def at(xx, yy, zz, cc):
        return (zz // 2, xx * 4 + yy, (zz % 2) * 2 + cc)

    def plane(dx, dy):
        return at((x + dx) % 4, (y + dy) % 4, z, core)

    partner = at(x, y, z, 1 - core)
    far = at(x, y, (z + sign + 8) % 8, core)
    near = at(x, y, (z - sign + 8) % 8, core)

    def remote(src, dst, send, recv, device):
        return pltpu.make_async_remote_copy(
            src_ref=src, dst_ref=dst, send_sem=send, recv_sem=recv,
            device_id=device, device_id_type=MESH,
        )

    local = [
        pltpu.make_async_copy(src.at[pl.ds(BLOCK * half, BLOCK)], tc.at[t, half, pl.ds(0, BLOCK)], loc_sem.at[2 * t + half])
        for t, src in enumerate((tok, cot))
        for half in range(2)
    ]
    local += [
        pltpu.make_async_copy(wg, wgu.at[0], loc_sem.at[4]),
        pltpu.make_async_copy(wu, wgu.at[1], loc_sem.at[5]),
        pltpu.make_async_copy(wd, wdn, loc_sem.at[6]),
    ]
    for copy in local:
        copy.start()
    barrier = pltpu.get_barrier_semaphore()

    neighbours = (partner, far, near, plane(1, 0), plane(3, 0), plane(0, 1), plane(0, 3))
    for device in neighbours:
        pl.semaphore_signal(barrier, inc=1, device_id=device, device_id_type=MESH)
    pl.semaphore_wait(barrier, len(neighbours))

    east, west = plane(1, 0), plane(3, 0)
    north, south = plane(0, 1), plane(0, 3)

    def block(t, k):
        rows = pl.ds(BLOCK * k, BLOCK)
        return tc.at[:, :, rows] if t is None else tc.at[t, :, rows]

    hops = (
        (0, 0, 14, east), (0, 0, 1, west), (0, 0, 15, north), (0, 0, 2, south),
        (0, 14, 3, east), (1, 1, 3, west),
        (None, 1, 6, north), (None, 14, 5, north), (None, 14, 4, south), (None, 1, 13, south),
        (0, 15, 9, north), (1, 2, 9, south),
        (None, 3, 8, north), (None, 3, 7, south),
        (0, 6, 10, north), (1, 13, 10, south), (0, 5, 11, north), (1, 4, 11, south),
        (0, 8, 12, north), (1, 7, 12, south),
        (1, 0, 14, east), (1, 0, 1, west), (1, 0, 15, north), (1, 0, 2, south),
    )
    a1 = [
        remote(block(t, src), block(t, dst), a_send.at[n], a_recv.at[n], device)
        for n, (t, src, dst, device) in enumerate(hops)
    ]

    def tokens_in(*numbers):
        for n in numbers:
            a1[n].wait_recv()

    def tokens_out(*numbers):
        for n in numbers:
            a1[n].start()

    weights = [
        remote(wg, wgux.at[0], w_send.at[0], w_recv.at[0], partner),
        remote(wu, wgux.at[1], w_send.at[1], w_recv.at[1], partner),
        remote(wd, wdnx, w_send.at[2], w_recv.at[2], partner),
    ]
    for copy in local[:4]:
        copy.wait()
    tokens_out(0, 1, 2, 3, 20, 21, 22, 23)
    for copy in weights:
        copy.start()
    sums = (accg, accu, accd)
    for total in sums:
        total[...] = jnp.zeros_like(total)
    for copy in local[4:]:
        copy.wait()

    def stage_rows(s):
        return pl.ds(pl.multiple_of(s * ROWS, ROWS), ROWS)

    def swap(s, t):
        rows = stage_rows(s)
        return remote(tc.at[t, 1 - core, rows], tx.at[t, rows], x_send.at[s, t], x_recv.at[s, t], partner)

    def forward_in(s):
        swap(s, 0).wait_recv()
        slot = s % 3
        mine, other = tc[0, core, stage_rows(s), :], tx[0, stage_rows(s), :]
        for t in range(2):
            q[slot, :, t * ff : (t + 1) * ff] = jnp.dot(
                mine, wgu[t], preferred_element_type=F32
            ) + jnp.dot(other, wgux[t], preferred_element_type=F32)

    def forward_out(s):
        swap(s, 1).wait_recv()
        slot = s % 3
        mine, other = tc[1, core, stage_rows(s), :], tx[1, stage_rows(s), :]
        dims = (((1,), (1,)), ((), ()))
        q[slot, :, 2 * ff :] = lax.dot_general(
            mine, wdn[...], dims, preferred_element_type=F32
        ) + lax.dot_general(other, wdnx[...], dims, preferred_element_type=F32)

    def chunk(o):
        return pl.ds(pl.multiple_of(((o + 16) % 8) * CHUNK, CHUNK), CHUNK)

    def part_of(ref, p):
        return ref.at[:, pl.ds(*PARTS[p])]

    def sum_long(s, h, p):
        return remote(
            part_of(sl.at[s, h - 1], p), part_of(rl.at[s, h - 1], p), ring_send.at[0], rl_recv.at[s, h - 1, p], far
        )

    def sum_short(s, h, p):
        return remote(
            part_of(ss.at[s, h - 1], p), part_of(rs.at[s, h - 1], p), ring_send.at[1], rs_recv.at[s, h - 1, p], near
        )

    def sum_send(s, h, p):
        cols = pl.ds(*PARTS[p])
        part = q[s % 3, chunk(z + (5 - h) * sign), cols]
        if h > 1:
            part = part + rl[s, h - 2, :, cols].astype(F32)
        sl[s, h - 1, :, cols] = part.astype(BF16)
        sum_long(s, h, p).start()
        if h < 4:
            part = q[s % 3, chunk(z - (4 - h) * sign), cols]
            if h > 1:
                part = part + rs[s, h - 2, :, cols].astype(F32)
            ss[s, h - 1, :, cols] = part.astype(BF16)
            sum_short(s, h, p).start()

    def sum_wait(s, h, p):
        sum_long(s, h, p).wait_recv()
        if h < 4:
            sum_short(s, h, p).wait_recv()

    def sum_on(s, h):
        for p in range(2):
            sum_wait(s, h, p)
            sum_send(s, h + 1, p)

    def piece_of(s, o):
        return hid.at[s, core, chunk(o)]

    def spread_long(s, o, h, p):
        piece = part_of(piece_of(s, o), p)
        return remote(piece, piece, ring_send.at[2], al_recv.at[s, h - 1, p], far)

    def spread_short(s, o, h, p):
        piece = part_of(piece_of(s, o), p)
        return remote(piece, piece, ring_send.at[3], as_recv.at[s, h - 1, p], near)

    def pass_on(s, o):
        piece = piece_of(s, o)
        remote(piece, piece, pf_send.at[0], pf_recv.at[s], partner).start()

    def spread_send(s, h, p):
        spread_long(s, z - (h - 1) * sign, h, p).start()
        if h < 4:
            spread_short(s, z + (h - 1) * sign, h, p).start()

    def spread_wait(s, h, p):
        spread_long(s, z - h * sign, h, p).wait_recv()
        if h < 4:
            spread_short(s, z + h * sign, h, p).wait_recv()

    def spread_on(s, h):
        for p in range(2):
            spread_wait(s, h, p)
            if h < 4:
                spread_send(s, h + 1, p)
        pass_on(s, z - h * sign)
        if h < 4:
            pass_on(s, z + h * sign)

    def pointwise(s):
        total = q[s % 3, chunk(z), :] + rl[s, 3].astype(F32) + rs[s, 2].astype(F32)
        gate, up, back = total[:, :ff], total[:, ff : 2 * ff], total[:, 2 * ff :]
        sig = jax.nn.sigmoid(gate)
        piece = chunk(z)
        hid[s, core, piece, 0:ff] = (gate * sig * up).astype(BF16)
        hid[s, core, piece, ff : 2 * ff] = (back * up * sig * (1.0 + gate * (1.0 - sig))).astype(BF16)
        hid[s, core, piece, 2 * ff :] = (back * gate * sig).astype(BF16)

    def both_halves(s):
        theirs = hid.at[s, 1 - core]
        return remote(theirs, theirs, pf_send.at[0], pf_recv.at[s], partner)

    def stage_hidden(s, t):
        return hid[s, :, :, t * ff : (t + 1) * ff].reshape(2 * ROWS, ff)

    def stage_tokens(s, t):
        return tc[t, :, stage_rows(s), :].reshape(2 * ROWS, tc.shape[-1])

    def block_copy(k, half):
        rows = pl.ds(BLOCK * k, BLOCK)
        late = k >= LATE
        return remote(igb.at[half, rows], igr.at[k, half], ig_send.at[int(late)], ig_recv.at[int(late)], plane(*PLACES[k]))

    def half_grad(s, half):
        dims = (((1,), (1,)), ((), ()))
        block = lax.dot_general(hid[s, half, :, ff : 2 * ff], wgu[0], dims, preferred_element_type=F32)
        block = block + lax.dot_general(hid[s, half, :, 2 * ff :], wgu[1], dims, preferred_element_type=F32)
        igb[half, stage_rows(s), :] = block.astype(BF16)

        for stage in range(STAGES):

            @pl.when(s == stage)
            def _():
                for k in range(max(1, ROWS * stage // BLOCK), ROWS * (stage + 1) // BLOCK):
                    block_copy(k, half).start()

    def input_grad(s):
        half_grad(s, core)
        both_halves(s).wait_recv()
        half_grad(s, 1 - core)

    outer = (((0,), (0,)), ((), ()))

    def column_grads(s):
        left = stage_tokens(s, 0)
        for t, out in enumerate(sums[:2]):
            out[...] += lax.dot_general(left, stage_hidden(s, t + 1), outer, preferred_element_type=F32)

    def down_grad(s):
        accd[...] += lax.dot_general(stage_hidden(s, 0), stage_tokens(s, 1), outer, preferred_element_type=F32)

    tokens_in(0, 1, 2, 3)
    swap(0, 0).start()
    tokens_out(4)
    for copy in weights[:2]:
        copy.wait_recv()
    forward_in(0)
    sum_send(0, 1, 0)
    tokens_in(20, 21, 22, 23)
    swap(0, 1).start()
    tokens_out(5, 7, 8, 6, 9)
    weights[2].wait_recv()
    forward_out(0)
    sum_send(0, 1, 1)

    def step(i, carry):
        front = i < STAGES
        back = (i > 0) & (i < STAGES + 1)
        out_front = (i > 1) & (i < STAGES + 2)
        out_back = (i > 2) & (i < STAGES + 3)
        grads = i > 3
        more = i < STAGES - 1

        @pl.when(i == 0)
        def _():
            tokens_in(4, 5)
            tokens_out(12, 13, 10, 11)
            tokens_in(7, 8)
            swap(1, 0).start()
            swap(1, 1).start()

        @pl.when(back)
        def _():
            sum_on(i - 1, 2)

        @pl.when(out_back)
        def _():
            spread_on(i - 3, 2)

        @pl.when(front)
        def _():
            sum_on(i, 1)

        @pl.when(grads)
        def _():
            input_grad(i - 4)

        @pl.when(i == 1)
        def _():
            tokens_in(6, 9)
            tokens_out(14, 15, 16, 17)
            tokens_in(12, 13)
            tokens_out(18, 19)

        @pl.when(i == 2)
        def _():
            tokens_in(10, 11, 14, 15)

        @pl.when(i == 3)
        def _():
            tokens_in(16, 17, 18, 19)

        @pl.when((i > 0) & more)
        def _():
            swap(i + 1, 0).start()
            swap(i + 1, 1).start()

        @pl.when(back)
        def _():
            sum_on(i - 1, 3)

        @pl.when(grads)
        def _():
            down_grad(i - 4)

        @pl.when(out_front)
        def _():
            spread_on(i - 2, 1)

        @pl.when(out_back)
        def _():
            spread_on(i - 3, 3)

        @pl.when(grads)
        def _():
            column_grads(i - 4)

        @pl.when(more)
        def _():
            forward_in(i + 1)
            sum_send(i + 1, 1, 0)
            forward_out(i + 1)
            sum_send(i + 1, 1, 1)

        @pl.when(back)
        def _():
            sum_wait(i - 1, 4, 0)
            sum_wait(i - 1, 4, 1)
            pointwise(i - 1)
            spread_send(i - 1, 1, 0)
            spread_send(i - 1, 1, 1)
            pass_on(i - 1, z)

        @pl.when(out_back)
        def _():
            spread_on(i - 3, 4)

        return carry

    lax.fori_loop(0, STAGES + 4, step, 0)

    for out, total in zip((gg_out, gu_out, gd_out), sums):
        out[...] = total[...].astype(BF16)

    def arrived(first, last, late):
        blocks = igr.at[pl.ds(first, last - first)]
        remote(blocks, blocks, ig_send.at[late], ig_recv.at[late], partner).wait()

    arrived(1, LATE, 0)
    total = igb[:, 0:BLOCK, :].astype(F32)
    for k in range(1, LATE):
        total = total + igr[k].astype(F32)
    arrived(LATE, 16, 1)
    for k in range(LATE, 16):
        total = total + igr[k].astype(F32)
    ig_out[...] = total.reshape(2 * BLOCK, total.shape[-1]).astype(BF16)

    for copy in a1 + weights:
        copy.wait_send()

    @pl.loop(0, STAGES)
    def _(s):
        swap(s, 0).wait_send()
        swap(s, 1).wait_send()

    remote(sl, sl, ring_send.at[0], ring_send.at[0], far).wait_send()
    remote(ss, ss, ring_send.at[1], ring_send.at[1], near).wait_send()
    remote(sl, sl, ring_send.at[2], ring_send.at[2], far).wait_send()
    remote(ss, ss, ring_send.at[3], ring_send.at[3], near).wait_send()
    mine = hid.at[:, core]
    remote(mine, mine, pf_send.at[0], pf_send.at[0], partner).wait_send()


def stored(*refs):
    copies = [pltpu.make_async_copy(refs[n], refs[4 + n], refs[8].at[n]) for n in range(4)]
    for copy in copies:
        copy.start()
    for copy in copies:
        copy.wait()


def on_device(tokens, cotangent, gate_weight, up_weight, down_weight):
    width, ff = gate_weight.shape
    DMA = pltpu.SemaphoreType.DMA
    hbm = pl.BlockSpec(memory_space=pltpu.HBM)
    vmem = pl.BlockSpec(memory_space=pltpu.VMEM)
    outs = pl.pallas_call(
        kernel,
        out_shape=(
            pltpu.VMEM(tokens.shape, BF16),
            pltpu.VMEM((width, ff), BF16),
            pltpu.VMEM((width, ff), BF16),
            pltpu.VMEM((ff, width), BF16),
        ),
        in_specs=[hbm] * 5,
        out_specs=(vmem,) * 4,
        scratch_shapes=[
            pltpu.VMEM((2, 2, HALF, width), BF16),
            pltpu.VMEM((2, HALF, width), BF16),
            pltpu.VMEM((2, width, ff), BF16),
            pltpu.VMEM((ff, width), BF16),
            pltpu.VMEM((2, width, ff), BF16),
            pltpu.VMEM((ff, width), BF16),
            pltpu.VMEM((3, ROWS, 3 * ff), F32),
            pltpu.VMEM((STAGES, 4, CHUNK, 3 * ff), BF16),
            pltpu.VMEM((STAGES, 4, CHUNK, 3 * ff), BF16),
            pltpu.VMEM((STAGES, 3, CHUNK, 3 * ff), BF16),
            pltpu.VMEM((STAGES, 3, CHUNK, 3 * ff), BF16),
            pltpu.VMEM((STAGES, 2, ROWS, 3 * ff), BF16),
            pltpu.VMEM((width, ff), F32),
            pltpu.VMEM((width, ff), F32),
            pltpu.VMEM((ff, width), F32),
            pltpu.VMEM((2, HALF, width), BF16),
            pltpu.VMEM((16, 2, BLOCK, width), BF16),
            DMA((7,)),
            DMA((3,)),
            DMA((3,)),
            DMA((24,)),
            DMA((24,)),
            DMA((STAGES, 2)),
            DMA((STAGES, 2)),
            DMA((4,)),
            DMA((STAGES, 4, 2)),
            DMA((STAGES, 3, 2)),
            DMA((STAGES, 4, 2)),
            DMA((STAGES, 3, 2)),
            DMA((1,)),
            DMA((STAGES,)),
            DMA((2,)),
            DMA((2,)),
        ],
        compiler_params=pltpu.CompilerParams(
            collective_id=0, has_side_effects=True, vmem_limit_bytes=64150000
        ),
    )(tokens, cotangent, gate_weight, up_weight, down_weight)
    outs = [pltpu.with_memory_space_constraint(out, pltpu.VMEM) for out in outs]
    return pl.pallas_call(
        stored,
        out_shape=tuple(jax.ShapeDtypeStruct(out.shape, BF16) for out in outs),
        in_specs=[vmem] * 4,
        out_specs=(hbm,) * 4,
        scratch_shapes=[DMA((4,))],
        compiler_params=pltpu.CompilerParams(vmem_limit_bytes=1024 * 1024),
    )(*outs)


def solution(mesh):
    return jax.shard_map(
        on_device,
        mesh=mesh,
        in_specs=(
            P("row", ("depth", "col")),
            P("row", ("depth", "col")),
            P(("depth", "col"), "row"),
            P(("depth", "col"), "row"),
            P("row", ("depth", "col")),
        ),
        out_specs=(
            P("row", ("depth", "col")),
            P(("depth", "col"), "row"),
            P(("depth", "col"), "row"),
            P("row", ("depth", "col")),
        ),
        check_vma=False,
    )
```
